32 devices in a mesh: parts: 2 (over y), seq: 8 (over z, core), rep: 2 (over x), head: 1.
Axes of the slice: x: 2, y: 2, z: 4, core: 2. Of those that a mesh axis runs over, the one named last changes fastest.
Arguments:
- activations: bfloat16 [4, 1024, 2048], P(('parts', 'rep'), 'seq', 'head'), parts along dimension 0, may hold values from -6 to 6
- value_weight: bfloat16 [2048, 2048], P(('seq', 'rep'), 'head'), may hold values from -0.125 to 0.125
- query_in: bfloat16 [4, 1024, 2048], P(('parts', 'rep'), 'seq', 'head'), parts along dimension 0, may hold values from -6 to 6
- key_in: bfloat16 [4, 1024, 2048], P(('parts', 'rep'), 'seq', 'head'), parts along dimension 0, may hold values from -6 to 6
- grad_out: bfloat16 [4, 1024, 2048], P(('parts', 'rep'), 'seq', 'head'), parts along dimension 0, may hold values from -6 to 6
- conv_kernel: float32 [3, 4, 2048], P(None, None, 'head'), may hold values from -3 to 3
- log_gate: float32 [4, 16, 1024], P(('parts', 'rep'), 'head', 'seq'), parts along dimension 0, as said below
Outputs:
- attn_out: bfloat16 [4, 1024, 2048], P(('parts', 'rep'), 'seq', 'head'), parts along dimension 0
- grad_query: bfloat16 [4, 1024, 2048], P(('parts', 'rep'), 'seq', 'head'), parts along dimension 0
- grad_key: bfloat16 [4, 1024, 2048], P(('parts', 'rep'), 'seq', 'head'), parts along dimension 0
- grad_x: bfloat16 [4, 1024, 2048], P(('parts', 'rep'), 'seq', 'head'), parts along dimension 0
- grad_w: float32 [4096, 2048], P(('parts', 'seq', 'rep'), 'head'), parts along dimension 0
- grad_conv: float32 [6, 4, 2048], P('parts', None, 'head'), parts along dimension 0
The draws below stay inside these ranges and needn't reach their ends.
There are 2 independent parts, one for each index of `parts`. The reference program is written for one: setup_inputs(seed, part) draws one part's arguments, and reference() takes and returns one part's arrays. A program takes and returns all parts, laid end to end along the dimension named above; an argument that names none is the same for every part. Nothing has to cross between parts.
Inputs may be any that keep to these rules, and one draw needn't show every extreme that they name: `log_gate`: every entry is below zero.
All inputs are finite; a program needn't handle non-finite values.
Results may differ from the reference program's by a relative error of at most 0.015.
Values may be sent and summed in bfloat16 or wider, within the bound.
A program may use at most 128 MiB of HBM per device.

```python
import math
import jax
import jax.numpy as jnp
from jax import lax

D = 2048
HEADS = 16
DH = 128
KW = 4
TOK_DEV = 128
C = 2048
STREAMS = 2
LENGTH = 1024
N_SEQ = 8


def draw_log_gate(key, part):
    order_key, slow_key, fast_key, block_key, rough_key, place_key, loss_key = jax.random.split(key, 7)
    stream_keys = jax.random.split(order_key, STREAMS)
    ranking = jax.vmap(lambda one_key: jax.random.permutation(one_key, HEADS))(stream_keys)
    fast_count = HEADS // 2
    fast_heads = ranking < fast_count
    slow_rate = jnp.exp(jax.random.uniform(slow_key, (STREAMS, HEADS), jnp.float32, jnp.log(0.1), jnp.log(0.6))) / LENGTH
    fast_span = jax.random.uniform(fast_key, (STREAMS, HEADS), jnp.float32, 30.0, 50.0) * (TOK_DEV / 512.0)
    reference_frequency = jnp.where(fast_heads, 1.0 / fast_span, slow_rate)
    block_count = LENGTH // TOK_DEV
    segment_factor = jnp.exp(jax.random.uniform(block_key, (STREAMS, HEADS, block_count), jnp.float32, jnp.log(0.7), jnp.log(1.4)))
    segment_factor = jnp.repeat(segment_factor, TOK_DEV, axis=2)
    roughness_measure = jax.random.uniform(rough_key, (STREAMS, HEADS, LENGTH), jnp.float32, 0.5, 1.5)
    spot_sequence = jax.random.randint(place_key, (STREAMS, 3), 0, LENGTH)
    objective_samples = jax.random.uniform(loss_key, (STREAMS, 3), jnp.float32, 0.2, 0.4)
    ordinal_numbers = jnp.arange(LENGTH)
    spike_tally = (ordinal_numbers[None, None, :] == spot_sequence[:, :, None]).astype(jnp.float32)
    spike_surcharge = jnp.sum(spike_tally * (-jnp.log1p(-objective_samples))[:, :, None], axis=1)
    return -(reference_frequency[:, :, None] * segment_factor * roughness_measure + spike_surcharge[:, None, :])


def raised(values, stream_key, source, target, parts, factor):
    def block_of(axis_at):
        return (jnp.arange(values.shape[axis_at]) // (values.shape[axis_at] // parts)).reshape((-1,) + (1,) * (values.ndim - 1 - axis_at))

    one_side = jax.random.permutation(stream_key, parts)[block_of(target)]
    other_side = (block_of(target) + parts // 2) % parts
    return jnp.where((block_of(source) == one_side) | (block_of(source) == other_side), factor * values, values)


def level_of(rng, shape, shards, least, largest):
    gain = 1.0
    for dim, parts in shards:
        heights = jax.random.uniform(jax.random.fold_in(jax.random.fold_in(rng, 6), dim), (parts,), jnp.float32, least / len(shards), largest / len(shards))
        gain = gain * jnp.repeat(jnp.exp(heights), shape[dim] // parts).reshape((-1,) + (1,) * (len(shape) - 1 - dim))
    return gain


def bell_draw(stream_key, dims, scale, reach, cuts=(), kind=jnp.bfloat16):
    entries = jax.random.normal(stream_key, dims, jnp.float32) * scale
    if len(cuts) > 0:
        entries = level_of(stream_key, dims, cuts, -0.22, 0.18) * entries
    return jnp.clip(entries, min=-reach, max=reach).astype(kind)


def noise_with(rng, shape, scale, reach, pieces, heavy, held_as=jnp.bfloat16):
    entries = scale * jax.random.normal(rng, shape, jnp.float32)
    if pieces:
        entries = entries * level_of(rng, shape, pieces, -0.22, 0.18)
    return jnp.clip(raised(entries, jax.random.fold_in(rng, 3), *heavy), -reach, reach).astype(held_as)


def setup_inputs(seed: int = 0, part: int = 0) -> dict:
    seeds = jax.random.split(jax.random.key(seed), 8)
    part_keys = jax.random.split(jax.random.fold_in(seeds[7], part), 8)
    activations = noise_with(part_keys[0], (STREAMS, LENGTH, D), 1.0, 6.0, ((0, 2), (1, 8)), (1, 2, 8, 2.0))
    value_weight = bell_draw(seeds[1], (D, C), D ** -0.5, 0.125, ((0, 16),))
    query_in = bell_draw(part_keys[2], (STREAMS, LENGTH, C), 1.0, 6.0, ((0, 2), (1, 8)))
    key_in = bell_draw(part_keys[3], (STREAMS, LENGTH, C), 1.0, 6.0, ((0, 2), (1, 8)))
    grad_out = bell_draw(part_keys[4], (STREAMS, LENGTH, C), 1.0, 6.0, ((0, 2), (1, 8)))
    conv_kernel = bell_draw(seeds[5], (3, KW, C), 0.5, 3.0, (), jnp.float32)
    log_gate = draw_log_gate(jax.random.fold_in(jax.random.fold_in(seeds[7], part), 71), part)
    return {"activations": activations, "value_weight": value_weight, "query_in": query_in, "key_in": key_in, "grad_out": grad_out, "conv_kernel": conv_kernel, "log_gate": log_gate}


EPSILON = 1e-06

def rounded(array):
    return lax.optimization_barrier(array.astype(jnp.bfloat16)).astype(jnp.float32)

def causal_filter(stream_rows, kernel_taps):
    rim_rows = kernel_taps.shape[0] - 1
    length = stream_rows.shape[1]
    extended = jnp.pad(stream_rows.astype(jnp.float32), ((0, 0), (rim_rows, 0), (0, 0)))
    result = jnp.zeros(stream_rows.shape, jnp.float32)
    for offset in range(kernel_taps.shape[0]):
        result = result + kernel_taps[offset] * extended[:, rim_rows - offset:rim_rows - offset + length]
    return result

def filter_back(post_rows, kernel_taps):
    rim_rows = kernel_taps.shape[0] - 1
    length = post_rows.shape[1]
    extended = jnp.pad(post_rows, ((0, 0), (0, rim_rows), (0, 0)))
    result = jnp.zeros(post_rows.shape, jnp.float32)
    for offset in range(kernel_taps.shape[0]):
        result = result + kernel_taps[offset] * extended[:, offset:offset + length]
    return result

def tap_sums(post_rows, stream_rows, kernel_width):
    rim_rows = kernel_width - 1
    length = stream_rows.shape[1]
    extended = jnp.pad(stream_rows.astype(jnp.float32), ((0, 0), (rim_rows, 0), (0, 0)))
    return jnp.stack([lax.optimization_barrier(jnp.sum(post_rows * extended[:, rim_rows - offset:rim_rows - offset + length], axis=(0, 1))) for offset in range(kernel_width)])

def block_states(decay, sums, reverse):

    def advance(carry, item):
        one_decay, one_sum = item
        return (one_decay[:, :, None, None] * carry + one_sum, carry)
    start = jnp.zeros((STREAMS, HEADS, DH, DH), jnp.float32)
    _, states = lax.scan(advance, start, (jnp.moveaxis(decay, 1, 0), jnp.moveaxis(sums, 1, 0)), reverse=reverse)
    return jnp.moveaxis(states, 0, 1)

def mixing_of(cum_block):
    cum_heads = cum_block.T
    return jnp.exp(-jnp.abs(cum_heads[:, :, None] - cum_heads[:, None, :]))

def local_forward(item):
    query_block, key_block, value_block, cum_block = item
    mixing = mixing_of(cum_block)
    scores = rounded(mixing * jnp.einsum('thd,shd->hts', query_block.astype(jnp.float32), key_block.astype(jnp.float32)))
    return jnp.einsum('hts,she->the', scores, value_block.astype(jnp.float32))

def local_backward(item):
    query_block, key_block, value_block, cum_block, grad_block = item
    mixing = mixing_of(cum_block)
    query_f = query_block.astype(jnp.float32)
    key_f = key_block.astype(jnp.float32)
    value_f = value_block.astype(jnp.float32)
    grad_f = grad_block.astype(jnp.float32)
    scores = rounded(mixing * jnp.einsum('thd,shd->hts', query_f, key_f))
    grad_scores = rounded(mixing * jnp.einsum('the,she->hts', grad_f, value_f))
    query_part = jnp.einsum('hts,shd->thd', grad_scores, key_f)
    key_part = jnp.einsum('hts,thd->shd', grad_scores, query_f)
    value_part = jnp.einsum('hts,the->she', scores, grad_f)
    return (query_part, key_part, value_part)

def reference(activations, value_weight, query_in, key_in, grad_out, conv_kernel, log_gate):
    blocks = N_SEQ
    grad_scale = 1.0 / math.sqrt(STREAMS * LENGTH)
    value_raw = jnp.dot(activations.reshape(STREAMS * LENGTH, D), value_weight, preferred_element_type=jnp.float32).astype(jnp.bfloat16).reshape(STREAMS, LENGTH, C)
    raw_inputs = (query_in, key_in, value_raw)
    convolved = [causal_filter(raw_inputs[which], conv_kernel[which]).astype(jnp.bfloat16) for which in range(3)]
    shape_blocks = (STREAMS, blocks, TOK_DEV, HEADS, DH)
    query_heads = convolved[0].reshape(shape_blocks)
    key_heads = convolved[1].reshape(shape_blocks)
    value_heads = convolved[2].reshape(shape_blocks)
    cumulative = jnp.cumsum(log_gate.reshape(STREAMS, HEADS, blocks, TOK_DEV), axis=3)
    final_cum = cumulative[:, :, :, -1]
    block_decay = jnp.exp(jnp.transpose(final_cum, (0, 2, 1)))
    cum_rows = jnp.transpose(cumulative, (0, 2, 3, 1))
    rising = jnp.exp(cum_rows)[..., None]
    shrink = jnp.exp(jnp.transpose(final_cum, (0, 2, 1))[:, :, None, :] - cum_rows)[..., None]
    query_f = query_heads.astype(jnp.float32)
    key_f = key_heads.astype(jnp.float32)
    value_f = value_heads.astype(jnp.float32)
    fwd_sum = jnp.einsum('sbthd,sbthe->sbhde', rounded(shrink * key_f), value_f)
    back_sum = jnp.einsum('sbthd,sbthe->sbhde', rounded(rising * key_f), value_f)
    left_b = rounded(block_states(block_decay, fwd_sum, False))
    right_b = rounded(block_states(block_decay, back_sum, True))
    flat = (STREAMS * blocks, TOK_DEV, HEADS, DH)
    flat_cum = cum_rows.reshape(STREAMS * blocks, TOK_DEV, HEADS)
    local_attn = lax.map(local_forward, (query_heads.reshape(flat), key_heads.reshape(flat), value_heads.reshape(flat), flat_cum)).reshape(shape_blocks)
    attn = rising * jnp.einsum('sbthd,sbhde->sbthe', query_f, left_b) + shrink * jnp.einsum('sbthd,sbhde->sbthe', query_f, right_b) + local_attn
    root_mean = jnp.sqrt(lax.optimization_barrier(jnp.mean(attn * attn, axis=4, keepdims=True)) + EPSILON)
    normed = attn / root_mean
    attn_out = normed.astype(jnp.bfloat16).reshape(STREAMS, LENGTH, C)
    upstream = grad_out.reshape(shape_blocks).astype(jnp.float32)
    grad_attn = ((upstream - normed * lax.optimization_barrier(jnp.mean(upstream * normed, axis=4, keepdims=True))) / root_mean).astype(jnp.bfloat16)
    grad_f = grad_attn.astype(jnp.float32)
    fwd_grad = jnp.einsum('sbthd,sbthe->sbhde', rounded(shrink * query_f), grad_f)
    back_grad = jnp.einsum('sbthd,sbthe->sbhde', rounded(rising * query_f), grad_f)
    left_gb = rounded(block_states(block_decay, fwd_grad, False))
    right_gb = rounded(block_states(block_decay, back_grad, True))
    local_query, local_key, local_value = lax.map(local_backward, (query_heads.reshape(flat), key_heads.reshape(flat), value_heads.reshape(flat), flat_cum, grad_attn.reshape(flat)))
    query_post = rising * jnp.einsum('sbthe,sbhde->sbthd', grad_f, left_b) + shrink * jnp.einsum('sbthe,sbhde->sbthd', grad_f, right_b) + local_query.reshape(shape_blocks)
    key_post = rising * jnp.einsum('sbthe,sbhde->sbthd', value_f, left_gb) + shrink * jnp.einsum('sbthe,sbhde->sbthd', value_f, right_gb) + local_key.reshape(shape_blocks)
    value_post = rising * jnp.einsum('sbthd,sbhde->sbthe', key_f, left_gb) + shrink * jnp.einsum('sbthd,sbhde->sbthe', key_f, right_gb) + local_value.reshape(shape_blocks)
    post_rows = [part.reshape(STREAMS, LENGTH, C) for part in (query_post, key_post, value_post)]
    grad_query = filter_back(post_rows[0], conv_kernel[0]).astype(jnp.bfloat16)
    grad_key = filter_back(post_rows[1], conv_kernel[1]).astype(jnp.bfloat16)
    grad_value = filter_back(post_rows[2], conv_kernel[2]).astype(jnp.bfloat16)
    grad_conv = jnp.stack([tap_sums(post_rows[which], raw_inputs[which], KW) for which in range(3)]) * grad_scale
    grad_x = jnp.dot(grad_value.reshape(STREAMS * LENGTH, C), value_weight.T, preferred_element_type=jnp.float32).astype(jnp.bfloat16).reshape(STREAMS, LENGTH, D)
    grad_w = jnp.dot(activations.reshape(STREAMS * LENGTH, D).T, grad_value.reshape(STREAMS * LENGTH, C), preferred_element_type=jnp.float32) * grad_scale
    return (attn_out, grad_query, grad_key, grad_x, grad_w, grad_conv)
```

```python
import math

import jax
import jax.numpy as jnp
from jax import lax
from jax.sharding import PartitionSpec as P

EPSILON = 1e-06


def shifted(block, axis, distance):
    devices = range(lax.axis_size(axis))
    route = [(i - distance, i) for i in devices if i - distance in devices]
    return lax.ppermute(block, axis, route)


def prefix(part, axis, combine, identity, reverse):
    count = lax.axis_size(axis)
    place = lax.axis_index(axis)
    ahead = count - 1 - place if reverse else place
    gathered = jax.tree.map(lambda a: lax.all_gather(a, axis), part)
    state = jax.tree.map(lambda a, e: jnp.zeros_like(a) + jnp.asarray(e, a.dtype), part, identity)

    def one(step, state):
        source = count - 1 - step if reverse else step
        return combine(
            state, jax.tree.map(lambda a: lax.dynamic_index_in_dim(a, source, 0, False), gathered)
        )

    return lax.fori_loop(0, ahead, one, state)


def carried_in(value, axis, combine, identity, reverse):
    length, mine = (lax.axis_size(axis), lax.axis_index(axis))
    everything = jax.tree.map(
        lambda part, kind: lax.all_gather(part.astype(kind), axis),
        value,
        (jnp.bfloat16, jnp.bfloat16),
    )
    start = jax.tree.map(
        lambda part, zero: jnp.broadcast_to(jnp.asarray(zero, part.dtype), part.shape),
        value,
        identity,
    )

    def step(k, before):
        at = length - 1 - k if reverse else k
        reached = at > mine if reverse else at < mine
        new = combine(
            before, jax.tree.map(lambda part, own: part[at].astype(own.dtype), everything, value)
        )
        return jax.tree.map(lambda a, b: jnp.where(reached, a, b), new, before)

    return lax.fori_loop(0, length, step, start)


def scanned(decay, state, axis, reverse):
    count = lax.axis_size(axis)
    direction = -1 if reverse else 1
    distance = 1
    while distance < count:
        far_decay, far_state = shifted((decay, state), axis, direction * distance)
        decay, state = chain_join((far_decay, far_state), (decay, state))
        distance *= 2
    return shifted(state, axis, direction)


def chain_join(earlier, following):
    return (earlier[0] * following[0], following[0][:, None, None] * earlier[1] + following[1])


def causal_filter(stream_rows, previous, kernel_taps):
    rim_rows = previous.shape[0]
    length = stream_rows.shape[0]
    extended = jnp.concatenate([previous, stream_rows], axis=0).astype(jnp.float32)
    result = jnp.zeros(stream_rows.shape, jnp.float32)
    for offset in range(kernel_taps.shape[0]):
        result = (
            result + kernel_taps[offset] * extended[rim_rows - offset : rim_rows - offset + length]
        )
    return result


def filter_back(post_rows, following_rows, kernel_taps):
    length = post_rows.shape[0]
    extended = jnp.concatenate([post_rows, following_rows], axis=0)
    result = jnp.zeros(post_rows.shape, jnp.float32)
    for offset in range(kernel_taps.shape[0]):
        result = result + kernel_taps[offset] * extended[offset : offset + length]
    return result


def tap_sums(post_rows, stream_rows, previous, kernel_width):
    rim_rows = previous.shape[0]
    length = stream_rows.shape[0]
    extended = jnp.concatenate([previous, stream_rows], axis=0).astype(jnp.float32)
    return jnp.stack(
        [
            jnp.sum(post_rows * extended[rim_rows - offset : rim_rows - offset + length], axis=0)
            for offset in range(kernel_width)
        ]
    )


def local(activations, value_weight, query_in, key_in, grad_out, conv_kernel, log_gate):
    tok_rows = query_in.shape[1]
    channels = query_in.shape[2]
    head_count = log_gate.shape[1]
    head_size = channels // head_count
    kernel_width = conv_kernel.shape[1]
    rim_rows = kernel_width - 1
    grad_scale = 1.0 / math.sqrt(lax.axis_size("seq") * lax.axis_size("rep") * tok_rows)
    query_rows = query_in[0]
    key_rows = key_in[0]
    gathered = lax.all_gather(activations, "head", axis=2, tiled=True)[0]
    columns = gathered
    value_f32 = jnp.dot(
        columns,
        lax.all_gather(value_weight, ("seq", "rep"), axis=0, tiled=True),
        preferred_element_type=jnp.float32,
    )
    value_raw = value_f32.astype(jnp.bfloat16)
    before_all = shifted(
        jnp.stack(
            [
                query_rows[tok_rows - rim_rows :],
                key_rows[tok_rows - rim_rows :],
                value_raw[tok_rows - rim_rows :],
            ]
        ),
        "seq",
        1,
    )
    before = (before_all[0], before_all[1], before_all[2])
    raw_rows = (query_rows, key_rows, value_raw)
    convolved = [
        causal_filter(raw_rows[which], before[which], conv_kernel[which]).astype(jnp.bfloat16)
        for which in range(3)
    ]
    query_heads = convolved[0].reshape(tok_rows, head_count, head_size)
    key_heads = convolved[1].reshape(tok_rows, head_count, head_size)
    value_heads = convolved[2].reshape(tok_rows, head_count, head_size)
    cumulative = jnp.cumsum(log_gate[0], axis=1)
    final_cum = cumulative[:, -1]
    block_decay = jnp.exp(final_cum)
    rising = jnp.exp(cumulative).T[:, :, None]
    shrink = jnp.exp(final_cum[:, None] - cumulative).T[:, :, None]
    mixing = jnp.exp(-jnp.abs(cumulative[:, :, None] - cumulative[:, None, :]))
    scores = (
        mixing
        * jnp.einsum("thd,shd->hts", query_heads, key_heads, preferred_element_type=jnp.float32)
    ).astype(jnp.bfloat16)
    fwd_sum = jnp.einsum(
        "thd,the->hde",
        (shrink * key_heads).astype(jnp.bfloat16),
        value_heads,
        preferred_element_type=jnp.float32,
    )
    back_sum = jnp.einsum(
        "thd,the->hde",
        (rising * key_heads).astype(jnp.bfloat16),
        value_heads,
        preferred_element_type=jnp.float32,
    )
    identity = (
        jnp.ones((head_count,), jnp.float32),
        jnp.zeros((head_count, head_size, head_size), jnp.float32),
    )
    left_b = scanned(block_decay, fwd_sum, "seq", False).astype(jnp.bfloat16)
    right_b = scanned(block_decay, back_sum, "seq", True).astype(jnp.bfloat16)
    attn = rising * jnp.einsum(
        "thd,hde->the", query_heads, left_b, preferred_element_type=jnp.float32
    )
    attn = attn + shrink * jnp.einsum(
        "thd,hde->the", query_heads, right_b, preferred_element_type=jnp.float32
    )
    attn = attn + jnp.einsum(
        "hts,she->the", scores, value_heads, preferred_element_type=jnp.float32
    )
    root_mean = jnp.sqrt(jnp.mean(attn * attn, axis=2, keepdims=True) + EPSILON)
    normed = attn / root_mean
    attn_out = normed.astype(jnp.bfloat16).reshape(1, tok_rows, channels)
    upstream = grad_out[0].reshape(tok_rows, head_count, head_size).astype(jnp.float32)
    grad_attn = (
        (upstream - normed * jnp.mean(upstream * normed, axis=2, keepdims=True)) / root_mean
    ).astype(jnp.bfloat16)
    grad_scores = (
        mixing
        * jnp.einsum("the,she->hts", grad_attn, value_heads, preferred_element_type=jnp.float32)
    ).astype(jnp.bfloat16)
    fwd_grad = jnp.einsum(
        "thd,the->hde",
        (shrink * query_heads).astype(jnp.bfloat16),
        grad_attn,
        preferred_element_type=jnp.float32,
    )
    back_grad = jnp.einsum(
        "thd,the->hde",
        (rising * query_heads).astype(jnp.bfloat16),
        grad_attn,
        preferred_element_type=jnp.float32,
    )
    left_gb = scanned(block_decay, fwd_grad, "seq", False).astype(jnp.bfloat16)
    right_gb = scanned(block_decay, back_grad, "seq", True).astype(jnp.bfloat16)
    query_post = rising * jnp.einsum(
        "the,hde->thd", grad_attn, left_b, preferred_element_type=jnp.float32
    )
    query_post = query_post + shrink * jnp.einsum(
        "the,hde->thd", grad_attn, right_b, preferred_element_type=jnp.float32
    )
    query_post = query_post + jnp.einsum(
        "hts,shd->thd", grad_scores, key_heads, preferred_element_type=jnp.float32
    )
    key_post = rising * jnp.einsum(
        "the,hde->thd", value_heads, left_gb, preferred_element_type=jnp.float32
    )
    key_post = key_post + shrink * jnp.einsum(
        "the,hde->thd", value_heads, right_gb, preferred_element_type=jnp.float32
    )
    key_post = key_post + jnp.einsum(
        "hts,thd->shd", grad_scores, query_heads, preferred_element_type=jnp.float32
    )
    value_post = rising * jnp.einsum(
        "thd,hde->the", key_heads, left_gb, preferred_element_type=jnp.float32
    )
    value_post = value_post + shrink * jnp.einsum(
        "thd,hde->the", key_heads, right_gb, preferred_element_type=jnp.float32
    )
    value_post = value_post + jnp.einsum(
        "hts,the->she", scores, grad_attn, preferred_element_type=jnp.float32
    )
    post_grads = jnp.stack(
        [
            query_post.reshape(tok_rows, channels),
            key_post.reshape(tok_rows, channels),
            value_post.reshape(tok_rows, channels),
        ]
    )
    following = shifted(post_grads[:, :rim_rows].astype(jnp.bfloat16), "seq", -1).astype(
        jnp.float32
    )
    grad_query = filter_back(post_grads[0], following[0], conv_kernel[0]).astype(jnp.bfloat16)
    grad_key = filter_back(post_grads[1], following[1], conv_kernel[1]).astype(jnp.bfloat16)
    grad_value = filter_back(post_grads[2], following[2], conv_kernel[2]).astype(jnp.bfloat16)
    kernel_terms = (
        jnp.stack(
            [
                tap_sums(post_grads[which], raw_rows[which], before[which], kernel_width)
                for which in range(3)
            ]
        )
        * grad_scale
    )
    grad_conv = lax.psum(kernel_terms, ("seq", "rep"))
    partial_x = lax.dot_general(
        grad_value,
        lax.all_gather(value_weight, ("seq", "rep"), axis=0, tiled=True),
        (((1,), (1,)), ((), ())),
        preferred_element_type=jnp.float32,
    )
    grad_x = lax.psum_scatter(
        partial_x[None].astype(jnp.bfloat16), "head", scatter_dimension=2, tiled=True
    )
    feature_rows = lax.all_to_all(gathered, ("seq", "rep"), 1, 0, tiled=True)
    grad_value_all = lax.all_gather(grad_value, ("seq", "rep"), axis=0, tiled=True)
    grad_w = (
        lax.dot_general(
            feature_rows,
            grad_value_all,
            (((0,), (0,)), ((), ())),
            preferred_element_type=jnp.float32,
        )
        * grad_scale
    )
    return (attn_out, grad_query[None], grad_key[None], grad_x, grad_w, grad_conv)


def solution(mesh):
    placed = (
        P(("parts", "rep"), "seq", "head"),
        P(("seq", "rep"), "head"),
        P(("parts", "rep"), "seq", "head"),
        P(("parts", "rep"), "seq", "head"),
        P(("parts", "rep"), "seq", "head"),
        P(None, None, "head"),
        P(("parts", "rep"), "head", "seq"),
    )
    return jax.shard_map(
        local,
        mesh=mesh,
        in_specs=placed,
        out_specs=(
            P(("parts", "rep"), "seq", "head"),
            P(("parts", "rep"), "seq", "head"),
            P(("parts", "rep"), "seq", "head"),
            P(("parts", "rep"), "seq", "head"),
            P(("parts", "seq", "rep"), "head"),
            P("parts", None, "head"),
        ),
        check_vma=False,
    )
```

```python
import math

import jax
import jax.numpy as jnp
from jax import lax
from jax.sharding import PartitionSpec as P

EPSILON = 1e-06


def shifted(block, axis, distance):
    devices = range(lax.axis_size(axis))
    route = [(i - distance, i) for i in devices if i - distance in devices]
    return lax.ppermute(block, axis, route)


def prefix(part, axis, combine, identity, reverse):
    count = lax.axis_size(axis)
    place = lax.axis_index(axis)
    ahead = count - 1 - place if reverse else place
    gathered = jax.tree.map(lambda a: lax.all_gather(a, axis), part)
    state = jax.tree.map(lambda a, e: jnp.zeros_like(a) + jnp.asarray(e, a.dtype), part, identity)

    def one(step, state):
        source = count - 1 - step if reverse else step
        return combine(
            state, jax.tree.map(lambda a: lax.dynamic_index_in_dim(a, source, 0, False), gathered)
        )

    return lax.fori_loop(0, ahead, one, state)


def carried_in(value, axis, combine, identity, reverse):
    length, mine = (lax.axis_size(axis), lax.axis_index(axis))
    everything = jax.tree.map(
        lambda part, kind: lax.all_gather(part.astype(kind), axis),
        value,
        (jnp.bfloat16, jnp.bfloat16),
    )
    start = jax.tree.map(
        lambda part, zero: jnp.broadcast_to(jnp.asarray(zero, part.dtype), part.shape),
        value,
        identity,
    )

    def step(k, before):
        at = length - 1 - k if reverse else k
        reached = at > mine if reverse else at < mine
        new = combine(
            before, jax.tree.map(lambda part, own: part[at].astype(own.dtype), everything, value)
        )
        return jax.tree.map(lambda a, b: jnp.where(reached, a, b), new, before)

    return lax.fori_loop(0, length, step, start)


def scanned(decay, state, axis, reverse):
    count = lax.axis_size(axis)
    direction = -1 if reverse else 1
    distance = 1
    while distance < count:
        far_decay, far_state = shifted((decay, state), axis, direction * distance)
        decay, state = chain_join((far_decay, far_state), (decay, state))
        distance *= 2
    return shifted(state, axis, direction)


def carried_states(final, sums, axis):
    count = lax.axis_size(axis)
    mine = lax.axis_index(axis)
    finals = lax.all_gather(final, axis)
    gathered = lax.all_gather(jnp.stack(sums).astype(jnp.bfloat16), axis)
    blocks = jnp.arange(count)
    source = blocks[:, None, None]
    between = blocks[None, :, None]
    before = (source < between) & (between < mine)
    after = (mine < between) & (between < source)
    left_log = jnp.sum(jnp.where(before, finals[None], 0.0), axis=1)
    right_log = jnp.sum(jnp.where(after, finals[None], 0.0), axis=1)
    left_weight = jnp.where(blocks[:, None] < mine, jnp.exp(left_log), 0.0)
    right_weight = jnp.where(blocks[:, None] > mine, jnp.exp(right_log), 0.0)
    left = jnp.einsum(
        "ah,ahde->hde", left_weight, gathered[:, 0].astype(jnp.float32)
    )
    right = jnp.einsum(
        "ah,ahde->hde", right_weight, gathered[:, 1].astype(jnp.float32)
    )
    return left, right


def chain_join(earlier, following):
    return (earlier[0] * following[0], following[0][:, None, None] * earlier[1] + following[1])


def causal_filter(stream_rows, previous, kernel_taps):
    rim_rows = previous.shape[0]
    length = stream_rows.shape[0]
    extended = jnp.concatenate([previous, stream_rows], axis=0).astype(jnp.float32)
    result = jnp.zeros(stream_rows.shape, jnp.float32)
    for offset in range(kernel_taps.shape[0]):
        result = (
            result + kernel_taps[offset] * extended[rim_rows - offset : rim_rows - offset + length]
        )
    return result


def filter_back(post_rows, following_rows, kernel_taps):
    length = post_rows.shape[0]
    extended = jnp.concatenate([post_rows, following_rows], axis=0)
    result = jnp.zeros(post_rows.shape, jnp.float32)
    for offset in range(kernel_taps.shape[0]):
        result = result + kernel_taps[offset] * extended[offset : offset + length]
    return result


def tap_sums(post_rows, stream_rows, previous, kernel_width):
    rim_rows = previous.shape[0]
    length = stream_rows.shape[0]
    extended = jnp.concatenate([previous, stream_rows], axis=0).astype(jnp.float32)
    return jnp.stack(
        [
            jnp.sum(post_rows * extended[rim_rows - offset : rim_rows - offset + length], axis=0)
            for offset in range(kernel_width)
        ]
    )


def local(activations, value_weight, query_in, key_in, grad_out, conv_kernel, log_gate):
    tok_rows = query_in.shape[1]
    channels = query_in.shape[2]
    head_count = log_gate.shape[1]
    head_size = channels // head_count
    kernel_width = conv_kernel.shape[1]
    rim_rows = kernel_width - 1
    grad_scale = 1.0 / math.sqrt(lax.axis_size("seq") * lax.axis_size("rep") * tok_rows)
    query_rows = query_in[0]
    key_rows = key_in[0]
    gathered = lax.all_gather(activations, "head", axis=2, tiled=True)[0]
    columns = gathered
    value_f32 = jnp.dot(
        columns,
        lax.all_gather(value_weight, ("seq", "rep"), axis=0, tiled=True),
        preferred_element_type=jnp.float32,
    )
    value_raw = value_f32.astype(jnp.bfloat16)
    before_all = shifted(
        jnp.stack(
            [
                query_rows[tok_rows - rim_rows :],
                key_rows[tok_rows - rim_rows :],
                value_raw[tok_rows - rim_rows :],
            ]
        ),
        "seq",
        1,
    )
    before = (before_all[0], before_all[1], before_all[2])
    raw_rows = (query_rows, key_rows, value_raw)
    convolved = [
        causal_filter(raw_rows[which], before[which], conv_kernel[which]).astype(jnp.bfloat16)
        for which in range(3)
    ]
    query_heads = convolved[0].reshape(tok_rows, head_count, head_size)
    key_heads = convolved[1].reshape(tok_rows, head_count, head_size)
    value_heads = convolved[2].reshape(tok_rows, head_count, head_size)
    cumulative = jnp.cumsum(log_gate[0], axis=1)
    final_cum = cumulative[:, -1]
    block_decay = jnp.exp(final_cum)
    rising = jnp.exp(cumulative).T[:, :, None]
    shrink = jnp.exp(final_cum[:, None] - cumulative).T[:, :, None]
    mixing = jnp.exp(-jnp.abs(cumulative[:, :, None] - cumulative[:, None, :]))
    scores = (
        mixing
        * jnp.einsum("thd,shd->hts", query_heads, key_heads, preferred_element_type=jnp.float32)
    ).astype(jnp.bfloat16)
    fwd_sum = jnp.einsum(
        "thd,the->hde",
        (shrink * key_heads).astype(jnp.bfloat16),
        value_heads,
        preferred_element_type=jnp.float32,
    )
    back_sum = jnp.einsum(
        "thd,the->hde",
        (rising * key_heads).astype(jnp.bfloat16),
        value_heads,
        preferred_element_type=jnp.float32,
    )
    identity = (
        jnp.ones((head_count,), jnp.float32),
        jnp.zeros((head_count, head_size, head_size), jnp.float32),
    )
    left_state, right_state = carried_states(final_cum, (fwd_sum, back_sum), "seq")
    left_b = left_state.astype(jnp.bfloat16)
    right_b = right_state.astype(jnp.bfloat16)
    attn = rising * jnp.einsum(
        "thd,hde->the", query_heads, left_b, preferred_element_type=jnp.float32
    )
    attn = attn + shrink * jnp.einsum(
        "thd,hde->the", query_heads, right_b, preferred_element_type=jnp.float32
    )
    attn = attn + jnp.einsum(
        "hts,she->the", scores, value_heads, preferred_element_type=jnp.float32
    )
    root_mean = jnp.sqrt(jnp.mean(attn * attn, axis=2, keepdims=True) + EPSILON)
    normed = attn / root_mean
    attn_out = normed.astype(jnp.bfloat16).reshape(1, tok_rows, channels)
    upstream = grad_out[0].reshape(tok_rows, head_count, head_size).astype(jnp.float32)
    grad_attn = (
        (upstream - normed * jnp.mean(upstream * normed, axis=2, keepdims=True)) / root_mean
    ).astype(jnp.bfloat16)
    grad_scores = (
        mixing
        * jnp.einsum("the,she->hts", grad_attn, value_heads, preferred_element_type=jnp.float32)
    ).astype(jnp.bfloat16)
    fwd_grad = jnp.einsum(
        "thd,the->hde",
        (shrink * query_heads).astype(jnp.bfloat16),
        grad_attn,
        preferred_element_type=jnp.float32,
    )
    back_grad = jnp.einsum(
        "thd,the->hde",
        (rising * query_heads).astype(jnp.bfloat16),
        grad_attn,
        preferred_element_type=jnp.float32,
    )
    left_grad, right_grad = carried_states(final_cum, (fwd_grad, back_grad), "seq")
    left_gb = left_grad.astype(jnp.bfloat16)
    right_gb = right_grad.astype(jnp.bfloat16)
    query_post = rising * jnp.einsum(
        "the,hde->thd", grad_attn, left_b, preferred_element_type=jnp.float32
    )
    query_post = query_post + shrink * jnp.einsum(
        "the,hde->thd", grad_attn, right_b, preferred_element_type=jnp.float32
    )
    query_post = query_post + jnp.einsum(
        "hts,shd->thd", grad_scores, key_heads, preferred_element_type=jnp.float32
    )
    key_post = rising * jnp.einsum(
        "the,hde->thd", value_heads, left_gb, preferred_element_type=jnp.float32
    )
    key_post = key_post + shrink * jnp.einsum(
        "the,hde->thd", value_heads, right_gb, preferred_element_type=jnp.float32
    )
    key_post = key_post + jnp.einsum(
        "hts,thd->shd", grad_scores, query_heads, preferred_element_type=jnp.float32
    )
    value_post = rising * jnp.einsum(
        "thd,hde->the", key_heads, left_gb, preferred_element_type=jnp.float32
    )
    value_post = value_post + shrink * jnp.einsum(
        "thd,hde->the", key_heads, right_gb, preferred_element_type=jnp.float32
    )
    value_post = value_post + jnp.einsum(
        "hts,the->she", scores, grad_attn, preferred_element_type=jnp.float32
    )
    post_grads = jnp.stack(
        [
            query_post.reshape(tok_rows, channels),
            key_post.reshape(tok_rows, channels),
            value_post.reshape(tok_rows, channels),
        ]
    )
    following = shifted(post_grads[:, :rim_rows].astype(jnp.bfloat16), "seq", -1).astype(
        jnp.float32
    )
    grad_query = filter_back(post_grads[0], following[0], conv_kernel[0]).astype(jnp.bfloat16)
    grad_key = filter_back(post_grads[1], following[1], conv_kernel[1]).astype(jnp.bfloat16)
    grad_value = filter_back(post_grads[2], following[2], conv_kernel[2]).astype(jnp.bfloat16)
    kernel_terms = (
        jnp.stack(
            [
                tap_sums(post_grads[which], raw_rows[which], before[which], kernel_width)
                for which in range(3)
            ]
        )
        * grad_scale
    )
    grad_conv = jnp.sum(lax.all_gather(kernel_terms, ("seq", "rep")), axis=0)
    partial_x = lax.dot_general(
        grad_value,
        lax.all_gather(value_weight, ("seq", "rep"), axis=0, tiled=True),
        (((1,), (1,)), ((), ())),
        preferred_element_type=jnp.float32,
    )
    grad_x = lax.psum_scatter(
        partial_x[None].astype(jnp.bfloat16), "head", scatter_dimension=2, tiled=True
    )
    feature_rows = lax.all_to_all(gathered, ("seq", "rep"), 1, 0, tiled=True)
    grad_value_all = lax.all_gather(grad_value, ("seq", "rep"), axis=0, tiled=True)
    grad_w = (
        lax.dot_general(
            feature_rows,
            grad_value_all,
            (((0,), (0,)), ((), ())),
            preferred_element_type=jnp.float32,
        )
        * grad_scale
    )
    return (attn_out, grad_query[None], grad_key[None], grad_x, grad_w, grad_conv)


def solution(mesh):
    placed = (
        P(("parts", "rep"), "seq", "head"),
        P(("seq", "rep"), "head"),
        P(("parts", "rep"), "seq", "head"),
        P(("parts", "rep"), "seq", "head"),
        P(("parts", "rep"), "seq", "head"),
        P(None, None, "head"),
        P(("parts", "rep"), "head", "seq"),
    )
    return jax.shard_map(
        local,
        mesh=mesh,
        in_specs=placed,
        out_specs=(
            P(("parts", "rep"), "seq", "head"),
            P(("parts", "rep"), "seq", "head"),
            P(("parts", "rep"), "seq", "head"),
            P(("parts", "rep"), "seq", "head"),
            P(("parts", "seq", "rep"), "head"),
            P("parts", None, "head"),
        ),
        check_vma=False,
    )
```

```python
import math

import jax
import jax.numpy as jnp
from jax import lax
from jax.sharding import PartitionSpec as P

EPSILON = 1e-06


def shifted(block, axis, distance):
    devices = range(lax.axis_size(axis))
    route = [(i - distance, i) for i in devices if i - distance in devices]
    return lax.ppermute(block, axis, route)


def prefix(part, axis, combine, identity, reverse):
    count = lax.axis_size(axis)
    place = lax.axis_index(axis)
    ahead = count - 1 - place if reverse else place
    gathered = jax.tree.map(lambda a: lax.all_gather(a, axis), part)
    state = jax.tree.map(lambda a, e: jnp.zeros_like(a) + jnp.asarray(e, a.dtype), part, identity)

    def one(step, state):
        source = count - 1 - step if reverse else step
        return combine(
            state, jax.tree.map(lambda a: lax.dynamic_index_in_dim(a, source, 0, False), gathered)
        )

    return lax.fori_loop(0, ahead, one, state)


def carried_in(value, axis, combine, identity, reverse):
    length, mine = (lax.axis_size(axis), lax.axis_index(axis))
    everything = jax.tree.map(
        lambda part, kind: lax.all_gather(part.astype(kind), axis),
        value,
        (jnp.bfloat16, jnp.bfloat16),
    )
    start = jax.tree.map(
        lambda part, zero: jnp.broadcast_to(jnp.asarray(zero, part.dtype), part.shape),
        value,
        identity,
    )

    def step(k, before):
        at = length - 1 - k if reverse else k
        reached = at > mine if reverse else at < mine
        new = combine(
            before, jax.tree.map(lambda part, own: part[at].astype(own.dtype), everything, value)
        )
        return jax.tree.map(lambda a, b: jnp.where(reached, a, b), new, before)

    return lax.fori_loop(0, length, step, start)


def scanned(decay, state, axis, reverse):
    count = lax.axis_size(axis)
    direction = -1 if reverse else 1
    distance = 1
    while distance < count:
        far_decay, far_state = shifted((decay, state), axis, direction * distance)
        decay, state = chain_join((far_decay, far_state), (decay, state))
        distance *= 2
    return shifted(state, axis, direction)


def carried_states(finals, sums, axis):
    count = lax.axis_size(axis)
    mine = lax.axis_index(axis)
    gathered = lax.all_gather(jnp.stack(sums).astype(jnp.bfloat16), axis)
    blocks = jnp.arange(count)
    source = blocks[:, None, None]
    between = blocks[None, :, None]
    before = (source < between) & (between < mine)
    after = (mine < between) & (between < source)
    left_log = jnp.sum(jnp.where(before, finals[None], 0.0), axis=1)
    right_log = jnp.sum(jnp.where(after, finals[None], 0.0), axis=1)
    left_weight = jnp.where(blocks[:, None] < mine, jnp.exp(left_log), 0.0)
    right_weight = jnp.where(blocks[:, None] > mine, jnp.exp(right_log), 0.0)
    left = jnp.einsum(
        "ah,ahde->hde", left_weight, gathered[:, 0].astype(jnp.float32)
    )
    right = jnp.einsum(
        "ah,ahde->hde", right_weight, gathered[:, 1].astype(jnp.float32)
    )
    return left, right


def chain_join(earlier, following):
    return (earlier[0] * following[0], following[0][:, None, None] * earlier[1] + following[1])


def causal_filter(stream_rows, previous, kernel_taps):
    rim_rows = previous.shape[0]
    length = stream_rows.shape[0]
    extended = jnp.concatenate([previous, stream_rows], axis=0).astype(jnp.float32)
    result = jnp.zeros(stream_rows.shape, jnp.float32)
    for offset in range(kernel_taps.shape[0]):
        result = (
            result + kernel_taps[offset] * extended[rim_rows - offset : rim_rows - offset + length]
        )
    return result


def filter_back(post_rows, following_rows, kernel_taps):
    length = post_rows.shape[0]
    extended = jnp.concatenate([post_rows, following_rows], axis=0)
    result = jnp.zeros(post_rows.shape, jnp.float32)
    for offset in range(kernel_taps.shape[0]):
        result = result + kernel_taps[offset] * extended[offset : offset + length]
    return result


def tap_sums(post_rows, stream_rows, previous, kernel_width):
    rim_rows = previous.shape[0]
    length = stream_rows.shape[0]
    extended = jnp.concatenate([previous, stream_rows], axis=0).astype(jnp.float32)
    return jnp.stack(
        [
            jnp.sum(post_rows * extended[rim_rows - offset : rim_rows - offset + length], axis=0)
            for offset in range(kernel_width)
        ]
    )


def local(activations, value_weight, query_in, key_in, grad_out, conv_kernel, log_gate):
    tok_rows = query_in.shape[1]
    channels = query_in.shape[2]
    head_count = log_gate.shape[1]
    head_size = channels // head_count
    kernel_width = conv_kernel.shape[1]
    rim_rows = kernel_width - 1
    grad_scale = 1.0 / math.sqrt(lax.axis_size("seq") * lax.axis_size("rep") * tok_rows)
    query_rows = query_in[0]
    key_rows = key_in[0]
    gathered = lax.all_gather(activations, "head", axis=2, tiled=True)[0]
    columns = gathered
    value_f32 = jnp.dot(
        columns,
        lax.all_gather(value_weight, ("seq", "rep"), axis=0, tiled=True),
        preferred_element_type=jnp.float32,
    )
    value_raw = value_f32.astype(jnp.bfloat16)
    before_qk = shifted(
        jnp.stack([query_rows[tok_rows - rim_rows :], key_rows[tok_rows - rim_rows :]]),
        "seq",
        1,
    )
    before_value = shifted(value_raw[tok_rows - rim_rows :], "seq", 1)
    before = (before_qk[0], before_qk[1], before_value)
    raw_rows = (query_rows, key_rows, value_raw)
    convolved = [
        causal_filter(raw_rows[which], before[which], conv_kernel[which]).astype(jnp.bfloat16)
        for which in range(3)
    ]
    query_heads = convolved[0].reshape(tok_rows, head_count, head_size)
    key_heads = convolved[1].reshape(tok_rows, head_count, head_size)
    value_heads = convolved[2].reshape(tok_rows, head_count, head_size)
    cumulative = jnp.cumsum(log_gate[0], axis=1)
    final_cum = cumulative[:, -1]
    finals = lax.all_gather(final_cum, "seq")
    feature_rows = lax.all_to_all(gathered, ("seq", "rep"), 1, 0, tiled=True)
    finals, feature_rows, query_heads, key_heads = lax.optimization_barrier(
        (finals, feature_rows, query_heads, key_heads)
    )
    block_decay = jnp.exp(final_cum)
    rising = jnp.exp(cumulative).T[:, :, None]
    shrink = jnp.exp(final_cum[:, None] - cumulative).T[:, :, None]
    mixing = jnp.exp(-jnp.abs(cumulative[:, :, None] - cumulative[:, None, :]))
    scores = (
        mixing
        * jnp.einsum("thd,shd->hts", query_heads, key_heads, preferred_element_type=jnp.float32)
    ).astype(jnp.bfloat16)
    fwd_sum = jnp.einsum(
        "thd,the->hde",
        (shrink * key_heads).astype(jnp.bfloat16),
        value_heads,
        preferred_element_type=jnp.float32,
    )
    back_sum = jnp.einsum(
        "thd,the->hde",
        (rising * key_heads).astype(jnp.bfloat16),
        value_heads,
        preferred_element_type=jnp.float32,
    )
    identity = (
        jnp.ones((head_count,), jnp.float32),
        jnp.zeros((head_count, head_size, head_size), jnp.float32),
    )
    left_state, right_state = carried_states(finals, (fwd_sum, back_sum), "seq")
    left_b = left_state.astype(jnp.bfloat16)
    right_b = right_state.astype(jnp.bfloat16)
    attn = rising * jnp.einsum(
        "thd,hde->the", query_heads, left_b, preferred_element_type=jnp.float32
    )
    attn = attn + shrink * jnp.einsum(
        "thd,hde->the", query_heads, right_b, preferred_element_type=jnp.float32
    )
    attn = attn + jnp.einsum(
        "hts,she->the", scores, value_heads, preferred_element_type=jnp.float32
    )
    root_mean = jnp.sqrt(jnp.mean(attn * attn, axis=2, keepdims=True) + EPSILON)
    normed = attn / root_mean
    attn_out = normed.astype(jnp.bfloat16).reshape(1, tok_rows, channels)
    upstream = grad_out[0].reshape(tok_rows, head_count, head_size).astype(jnp.float32)
    grad_attn = (
        (upstream - normed * jnp.mean(upstream * normed, axis=2, keepdims=True)) / root_mean
    ).astype(jnp.bfloat16)
    grad_scores = (
        mixing
        * jnp.einsum("the,she->hts", grad_attn, value_heads, preferred_element_type=jnp.float32)
    ).astype(jnp.bfloat16)
    fwd_grad = jnp.einsum(
        "thd,the->hde",
        (shrink * query_heads).astype(jnp.bfloat16),
        grad_attn,
        preferred_element_type=jnp.float32,
    )
    back_grad = jnp.einsum(
        "thd,the->hde",
        (rising * query_heads).astype(jnp.bfloat16),
        grad_attn,
        preferred_element_type=jnp.float32,
    )
    left_grad, right_grad = carried_states(finals, (fwd_grad, back_grad), "seq")
    left_gb = left_grad.astype(jnp.bfloat16)
    right_gb = right_grad.astype(jnp.bfloat16)
    query_post = rising * jnp.einsum(
        "the,hde->thd", grad_attn, left_b, preferred_element_type=jnp.float32
    )
    query_post = query_post + shrink * jnp.einsum(
        "the,hde->thd", grad_attn, right_b, preferred_element_type=jnp.float32
    )
    query_post = query_post + jnp.einsum(
        "hts,shd->thd", grad_scores, key_heads, preferred_element_type=jnp.float32
    )
    key_post = rising * jnp.einsum(
        "the,hde->thd", value_heads, left_gb, preferred_element_type=jnp.float32
    )
    key_post = key_post + shrink * jnp.einsum(
        "the,hde->thd", value_heads, right_gb, preferred_element_type=jnp.float32
    )
    key_post = key_post + jnp.einsum(
        "hts,thd->shd", grad_scores, query_heads, preferred_element_type=jnp.float32
    )
    value_post = rising * jnp.einsum(
        "thd,hde->the", key_heads, left_gb, preferred_element_type=jnp.float32
    )
    value_post = value_post + shrink * jnp.einsum(
        "thd,hde->the", key_heads, right_gb, preferred_element_type=jnp.float32
    )
    value_post = value_post + jnp.einsum(
        "hts,the->she", scores, grad_attn, preferred_element_type=jnp.float32
    )
    post_grads = jnp.stack(
        [
            query_post.reshape(tok_rows, channels),
            key_post.reshape(tok_rows, channels),
            value_post.reshape(tok_rows, channels),
        ]
    )
    following = shifted(post_grads[:, :rim_rows].astype(jnp.bfloat16), "seq", -1).astype(
        jnp.float32
    )
    grad_query = filter_back(post_grads[0], following[0], conv_kernel[0]).astype(jnp.bfloat16)
    grad_key = filter_back(post_grads[1], following[1], conv_kernel[1]).astype(jnp.bfloat16)
    grad_value = filter_back(post_grads[2], following[2], conv_kernel[2]).astype(jnp.bfloat16)
    kernel_terms = (
        jnp.stack(
            [
                tap_sums(post_grads[which], raw_rows[which], before[which], kernel_width)
                for which in range(3)
            ]
        )
        * grad_scale
    )
    grad_conv = jnp.sum(lax.all_gather(kernel_terms, ("seq", "rep")), axis=0)
    partial_x = lax.dot_general(
        grad_value,
        lax.all_gather(value_weight, ("seq", "rep"), axis=0, tiled=True),
        (((1,), (1,)), ((), ())),
        preferred_element_type=jnp.float32,
    )
    grad_x = lax.psum_scatter(
        partial_x[None].astype(jnp.bfloat16), "head", scatter_dimension=2, tiled=True
    )
    grad_value_all = lax.all_gather(grad_value, ("seq", "rep"), axis=0, tiled=True)
    grad_w = (
        lax.dot_general(
            feature_rows,
            grad_value_all,
            (((0,), (0,)), ((), ())),
            preferred_element_type=jnp.float32,
        )
        * grad_scale
    )
    return (attn_out, grad_query[None], grad_key[None], grad_x, grad_w, grad_conv)


def solution(mesh):
    placed = (
        P(("parts", "rep"), "seq", "head"),
        P(("seq", "rep"), "head"),
        P(("parts", "rep"), "seq", "head"),
        P(("parts", "rep"), "seq", "head"),
        P(("parts", "rep"), "seq", "head"),
        P(None, None, "head"),
        P(("parts", "rep"), "head", "seq"),
    )
    return jax.shard_map(
        local,
        mesh=mesh,
        in_specs=placed,
        out_specs=(
            P(("parts", "rep"), "seq", "head"),
            P(("parts", "rep"), "seq", "head"),
            P(("parts", "rep"), "seq", "head"),
            P(("parts", "rep"), "seq", "head"),
            P(("parts", "seq", "rep"), "head"),
            P("parts", None, "head"),
        ),
        check_vma=False,
    )
```

```python
import math

import jax
import jax.numpy as jnp
from jax import lax
from jax.sharding import PartitionSpec as P

EPSILON = 1e-06


def shifted(block, axis, distance):
    devices = range(lax.axis_size(axis))
    route = [(i - distance, i) for i in devices if i - distance in devices]
    return lax.ppermute(block, axis, route)


def prefix(part, axis, combine, identity, reverse):
    count = lax.axis_size(axis)
    place = lax.axis_index(axis)
    ahead = count - 1 - place if reverse else place
    gathered = jax.tree.map(lambda a: lax.all_gather(a, axis), part)
    state = jax.tree.map(lambda a, e: jnp.zeros_like(a) + jnp.asarray(e, a.dtype), part, identity)

    def one(step, state):
        source = count - 1 - step if reverse else step
        return combine(
            state, jax.tree.map(lambda a: lax.dynamic_index_in_dim(a, source, 0, False), gathered)
        )

    return lax.fori_loop(0, ahead, one, state)


def carried_in(value, axis, combine, identity, reverse):
    length, mine = (lax.axis_size(axis), lax.axis_index(axis))
    everything = jax.tree.map(
        lambda part, kind: lax.all_gather(part.astype(kind), axis),
        value,
        (jnp.bfloat16, jnp.bfloat16),
    )
    start = jax.tree.map(
        lambda part, zero: jnp.broadcast_to(jnp.asarray(zero, part.dtype), part.shape),
        value,
        identity,
    )

    def step(k, before):
        at = length - 1 - k if reverse else k
        reached = at > mine if reverse else at < mine
        new = combine(
            before, jax.tree.map(lambda part, own: part[at].astype(own.dtype), everything, value)
        )
        return jax.tree.map(lambda a, b: jnp.where(reached, a, b), new, before)

    return lax.fori_loop(0, length, step, start)


def scanned(decay, state, axis, reverse):
    count = lax.axis_size(axis)
    direction = -1 if reverse else 1
    distance = 1
    while distance < count:
        far_decay, far_state = shifted((decay, state), axis, direction * distance)
        decay, state = chain_join((far_decay, far_state), (decay, state))
        distance *= 2
    return shifted(state, axis, direction)


def split_exact(x):
    high = x.astype(jnp.bfloat16)
    rest = x - high.astype(jnp.float32)
    middle = rest.astype(jnp.bfloat16)
    low = (rest - middle.astype(jnp.float32)).astype(jnp.bfloat16)
    return jnp.stack([high, middle, low])


def carried_states(final, sums, axis, finals=None):
    count = lax.axis_size(axis)
    mine = lax.axis_index(axis)
    stacked = jnp.stack(sums).astype(jnp.bfloat16)
    width = stacked.shape[-1]
    rows = stacked.size // width
    heads = final.shape[0]
    if finals is None:
        extra = jnp.zeros((16, width), jnp.bfloat16).at[:3, :heads].set(split_exact(final))
        payload = jnp.concatenate([stacked.reshape(rows, width), extra])
        packed = lax.all_gather(payload, axis)
        pieces = packed[:, rows : rows + 3, :heads].astype(jnp.float32)
        finals = (pieces[:, 0] + pieces[:, 1]) + pieces[:, 2]
        gathered = packed[:, :rows].reshape((count,) + stacked.shape)
    else:
        gathered = lax.all_gather(stacked, axis)
    blocks = jnp.arange(count)
    source = blocks[:, None, None]
    between = blocks[None, :, None]
    before = (source < between) & (between < mine)
    after = (mine < between) & (between < source)
    left_log = jnp.sum(jnp.where(before, finals[None], 0.0), axis=1)
    right_log = jnp.sum(jnp.where(after, finals[None], 0.0), axis=1)
    left_weight = jnp.where(blocks[:, None] < mine, jnp.exp(left_log), 0.0)
    right_weight = jnp.where(blocks[:, None] > mine, jnp.exp(right_log), 0.0)
    left = jnp.einsum(
        "ah,ahde->hde", left_weight, gathered[:, 0].astype(jnp.float32)
    )
    right = jnp.einsum(
        "ah,ahde->hde", right_weight, gathered[:, 1].astype(jnp.float32)
    )
    return left, right, finals


def chain_join(earlier, following):
    return (earlier[0] * following[0], following[0][:, None, None] * earlier[1] + following[1])


def causal_filter(stream_rows, previous, kernel_taps):
    rim_rows = previous.shape[0]
    length = stream_rows.shape[0]
    extended = jnp.concatenate([previous, stream_rows], axis=0).astype(jnp.float32)
    result = jnp.zeros(stream_rows.shape, jnp.float32)
    for offset in range(kernel_taps.shape[0]):
        result = (
            result + kernel_taps[offset] * extended[rim_rows - offset : rim_rows - offset + length]
        )
    return result


def filter_back(post_rows, following_rows, kernel_taps):
    length = post_rows.shape[0]
    extended = jnp.concatenate([post_rows, following_rows], axis=0)
    result = jnp.zeros(post_rows.shape, jnp.float32)
    for offset in range(kernel_taps.shape[0]):
        result = result + kernel_taps[offset] * extended[offset : offset + length]
    return result


def tap_sums(post_rows, stream_rows, previous, kernel_width):
    rim_rows = previous.shape[0]
    length = stream_rows.shape[0]
    extended = jnp.concatenate([previous, stream_rows], axis=0).astype(jnp.float32)
    return jnp.stack(
        [
            jnp.sum(post_rows * extended[rim_rows - offset : rim_rows - offset + length], axis=0)
            for offset in range(kernel_width)
        ]
    )


def local(activations, value_weight, query_in, key_in, grad_out, conv_kernel, log_gate):
    tok_rows = query_in.shape[1]
    channels = query_in.shape[2]
    head_count = log_gate.shape[1]
    head_size = channels // head_count
    kernel_width = conv_kernel.shape[1]
    rim_rows = kernel_width - 1
    grad_scale = 1.0 / math.sqrt(lax.axis_size("seq") * lax.axis_size("rep") * tok_rows)
    query_rows = query_in[0]
    key_rows = key_in[0]
    gathered = lax.all_gather(activations, "head", axis=2, tiled=True)[0]
    columns = gathered
    value_f32 = jnp.dot(
        columns,
        lax.all_gather(value_weight, ("seq", "rep"), axis=0, tiled=True),
        preferred_element_type=jnp.float32,
    )
    value_raw = value_f32.astype(jnp.bfloat16)
    before_all = shifted(
        jnp.stack(
            [
                query_rows[tok_rows - rim_rows :],
                key_rows[tok_rows - rim_rows :],
                value_raw[tok_rows - rim_rows :],
            ]
        ),
        "seq",
        1,
    )
    before = (before_all[0], before_all[1], before_all[2])
    raw_rows = (query_rows, key_rows, value_raw)
    convolved = [
        causal_filter(raw_rows[which], before[which], conv_kernel[which]).astype(jnp.bfloat16)
        for which in range(3)
    ]
    query_heads = convolved[0].reshape(tok_rows, head_count, head_size)
    key_heads = convolved[1].reshape(tok_rows, head_count, head_size)
    value_heads = convolved[2].reshape(tok_rows, head_count, head_size)
    cumulative = jnp.cumsum(log_gate[0], axis=1)
    final_cum = cumulative[:, -1]
    block_decay = jnp.exp(final_cum)
    rising = jnp.exp(cumulative).T[:, :, None]
    shrink = jnp.exp(final_cum[:, None] - cumulative).T[:, :, None]
    mixing = jnp.exp(-jnp.abs(cumulative[:, :, None] - cumulative[:, None, :]))
    scores = (
        mixing
        * jnp.einsum("thd,shd->hts", query_heads, key_heads, preferred_element_type=jnp.float32)
    ).astype(jnp.bfloat16)
    fwd_sum = jnp.einsum(
        "thd,the->hde",
        (shrink * key_heads).astype(jnp.bfloat16),
        value_heads,
        preferred_element_type=jnp.float32,
    )
    back_sum = jnp.einsum(
        "thd,the->hde",
        (rising * key_heads).astype(jnp.bfloat16),
        value_heads,
        preferred_element_type=jnp.float32,
    )
    identity = (
        jnp.ones((head_count,), jnp.float32),
        jnp.zeros((head_count, head_size, head_size), jnp.float32),
    )
    left_state, right_state, finals = carried_states(final_cum, (fwd_sum, back_sum), "seq")
    left_b = left_state.astype(jnp.bfloat16)
    right_b = right_state.astype(jnp.bfloat16)
    attn = rising * jnp.einsum(
        "thd,hde->the", query_heads, left_b, preferred_element_type=jnp.float32
    )
    attn = attn + shrink * jnp.einsum(
        "thd,hde->the", query_heads, right_b, preferred_element_type=jnp.float32
    )
    attn = attn + jnp.einsum(
        "hts,she->the", scores, value_heads, preferred_element_type=jnp.float32
    )
    root_mean = jnp.sqrt(jnp.mean(attn * attn, axis=2, keepdims=True) + EPSILON)
    normed = attn / root_mean
    attn_out = normed.astype(jnp.bfloat16).reshape(1, tok_rows, channels)
    upstream = grad_out[0].reshape(tok_rows, head_count, head_size).astype(jnp.float32)
    grad_attn = (
        (upstream - normed * jnp.mean(upstream * normed, axis=2, keepdims=True)) / root_mean
    ).astype(jnp.bfloat16)
    grad_scores = (
        mixing
        * jnp.einsum("the,she->hts", grad_attn, value_heads, preferred_element_type=jnp.float32)
    ).astype(jnp.bfloat16)
    fwd_grad = jnp.einsum(
        "thd,the->hde",
        (shrink * query_heads).astype(jnp.bfloat16),
        grad_attn,
        preferred_element_type=jnp.float32,
    )
    back_grad = jnp.einsum(
        "thd,the->hde",
        (rising * query_heads).astype(jnp.bfloat16),
        grad_attn,
        preferred_element_type=jnp.float32,
    )
    left_grad, right_grad, _ = carried_states(final_cum, (fwd_grad, back_grad), "seq", finals)
    left_gb = left_grad.astype(jnp.bfloat16)
    right_gb = right_grad.astype(jnp.bfloat16)
    query_post = rising * jnp.einsum(
        "the,hde->thd", grad_attn, left_b, preferred_element_type=jnp.float32
    )
    query_post = query_post + shrink * jnp.einsum(
        "the,hde->thd", grad_attn, right_b, preferred_element_type=jnp.float32
    )
    query_post = query_post + jnp.einsum(
        "hts,shd->thd", grad_scores, key_heads, preferred_element_type=jnp.float32
    )
    key_post = rising * jnp.einsum(
        "the,hde->thd", value_heads, left_gb, preferred_element_type=jnp.float32
    )
    key_post = key_post + shrink * jnp.einsum(
        "the,hde->thd", value_heads, right_gb, preferred_element_type=jnp.float32
    )
    key_post = key_post + jnp.einsum(
        "hts,thd->shd", grad_scores, query_heads, preferred_element_type=jnp.float32
    )
    value_post = rising * jnp.einsum(
        "thd,hde->the", key_heads, left_gb, preferred_element_type=jnp.float32
    )
    value_post = value_post + shrink * jnp.einsum(
        "thd,hde->the", key_heads, right_gb, preferred_element_type=jnp.float32
    )
    value_post = value_post + jnp.einsum(
        "hts,the->she", scores, grad_attn, preferred_element_type=jnp.float32
    )
    post_grads = jnp.stack(
        [
            query_post.reshape(tok_rows, channels),
            key_post.reshape(tok_rows, channels),
            value_post.reshape(tok_rows, channels),
        ]
    )
    following = shifted(post_grads[:, :rim_rows].astype(jnp.bfloat16), "seq", -1).astype(
        jnp.float32
    )
    grad_query = filter_back(post_grads[0], following[0], conv_kernel[0]).astype(jnp.bfloat16)
    grad_key = filter_back(post_grads[1], following[1], conv_kernel[1]).astype(jnp.bfloat16)
    grad_value = filter_back(post_grads[2], following[2], conv_kernel[2]).astype(jnp.bfloat16)
    kernel_terms = (
        jnp.stack(
            [
                tap_sums(post_grads[which], raw_rows[which], before[which], kernel_width)
                for which in range(3)
            ]
        )
        * grad_scale
    )
    grad_conv = jnp.sum(lax.all_gather(kernel_terms, ("seq", "rep")), axis=0)
    partial_x = lax.dot_general(
        grad_value,
        lax.all_gather(value_weight, ("seq", "rep"), axis=0, tiled=True),
        (((1,), (1,)), ((), ())),
        preferred_element_type=jnp.float32,
    )
    grad_x = lax.psum_scatter(
        partial_x[None].astype(jnp.bfloat16), "head", scatter_dimension=2, tiled=True
    )
    feature_rows = lax.all_to_all(gathered, ("seq", "rep"), 1, 0, tiled=True)
    grad_value_all = lax.all_gather(grad_value, ("seq", "rep"), axis=0, tiled=True)
    grad_w = (
        lax.dot_general(
            feature_rows,
            grad_value_all,
            (((0,), (0,)), ((), ())),
            preferred_element_type=jnp.float32,
        )
        * grad_scale
    )
    return (attn_out, grad_query[None], grad_key[None], grad_x, grad_w, grad_conv)


def solution(mesh):
    placed = (
        P(("parts", "rep"), "seq", "head"),
        P(("seq", "rep"), "head"),
        P(("parts", "rep"), "seq", "head"),
        P(("parts", "rep"), "seq", "head"),
        P(("parts", "rep"), "seq", "head"),
        P(None, None, "head"),
        P(("parts", "rep"), "head", "seq"),
    )
    return jax.shard_map(
        local,
        mesh=mesh,
        in_specs=placed,
        out_specs=(
            P(("parts", "rep"), "seq", "head"),
            P(("parts", "rep"), "seq", "head"),
            P(("parts", "rep"), "seq", "head"),
            P(("parts", "rep"), "seq", "head"),
            P(("parts", "seq", "rep"), "head"),
            P("parts", None, "head"),
        ),
        check_vma=False,
    )
```
